32 devices in a mesh: ctx: 16 (over z, y, x), tp: 2 (over core).
Axes of the slice: x: 2, y: 2, z: 4, core: 2. Of those that a mesh axis runs over, the one named last changes fastest.
Arguments:
- queries: bfloat16 [2048, 4096], P('ctx', 'tp'), may hold values from -220 to 220
- keys: bfloat16 [2048, 1024], P('ctx', 'tp'), may hold values from -6 to 6
- values: bfloat16 [2048, 1024], P('ctx', 'tp'), may hold values from -6 to 6
- out_weight: bfloat16 [4096, 4096], P('tp'), may hold values from -0.09375 to 0.09375
- residual: bfloat16 [2048, 4096], P('ctx', 'tp'), may hold values from -1.5 to 1.5
- norm_gain: bfloat16 [4096], P('tp'), may hold values from 0.5 to 1.5
- span_order: int32 [32], replicated, may hold values from 0 to 31, as said below
Outputs:
- normed: bfloat16 [2048, 4096], P('ctx', 'tp')
The draws below stay inside these ranges and needn't reach their ends.
Inputs may be any that keep to these rules, and one draw needn't show every extreme that they name: `span_order`: every span appears in exactly one slot. The two slots of one index d of ctx (slots 2d and 2d + 1) hold a span p and its mirror, the span at the same place counted from the end of the sequence; which index holds which pair, and the order of the two, are drawn.
All inputs are finite; a program needn't handle non-finite values.
Results may differ from the reference program's by a relative error of at most 0.009.
Values may be sent and summed in bfloat16 or wider, within the bound.
A program may use at most 64 MiB of HBM per device.

```python
import math
import jax
import jax.numpy as jnp
from jax import lax

D = 4096
QUERY_HEADS = 32
KEY_VALUE_HEADS = 8
HEAD_SIZE = 128
SEQUENCE_LENGTH = 2048
N_CTX = 16


def paired_draw(key):
    base = jax.random.fold_in(key, 4242)
    query_key, random_key_seed = jax.random.split(base)
    query_raw = jnp.clip(jax.random.normal(query_key, (SEQUENCE_LENGTH, QUERY_HEADS, HEAD_SIZE), jnp.float32), -6.0, 6.0)
    key_input_rows = jnp.clip(jax.random.normal(random_key_seed, (SEQUENCE_LENGTH, KEY_VALUE_HEADS, HEAD_SIZE), jnp.float32), -6.0, 6.0)
    key_output_rows = key_input_rows
    query_output_rows = query_raw
    return (query_output_rows.reshape(SEQUENCE_LENGTH, QUERY_HEADS * HEAD_SIZE), key_output_rows.reshape(SEQUENCE_LENGTH, KEY_VALUE_HEADS * HEAD_SIZE))


def draw_queries(key, part):
    return paired_draw(key)[0].astype(jnp.bfloat16)


def draw_keys(key, part):
    return paired_draw(key)[1].astype(jnp.bfloat16)


def draw_span_order(key, part):
    base = jax.random.fold_in(key, 7171)
    order_key, flip_key = jax.random.split(base)
    pairs = jax.random.permutation(order_key, jnp.arange(N_CTX, dtype=jnp.int32))
    mirror = 2 * N_CTX - 1 - pairs
    flipped = jax.random.randint(flip_key, (N_CTX,), 0, 2, dtype=jnp.int32)
    first = jnp.where(flipped == 1, mirror, pairs)
    second = jnp.where(flipped == 1, pairs, mirror)
    return jnp.stack([first, second], axis=1).reshape(2 * N_CTX).astype(jnp.int32)


def block_scale(stream_key, shape, cuts, smallest, high):
    gain, own = 1.0, jax.random.fold_in(stream_key, 6)
    for dim, blocks in cuts:
        heights = jnp.exp(jax.random.uniform(jax.random.fold_in(own, dim), (blocks,), jnp.float32, smallest / len(cuts), high / len(cuts)))
        gain = gain * jnp.repeat(heights, shape[dim] // blocks).reshape([-1 if axis == dim else 1 for axis in range(len(shape))])
    return gain


def scatter_about(rng, extent, spread, most, pieces=(), kind=jnp.bfloat16):
    result = spread * jax.random.normal(rng, extent, jnp.float32)
    if pieces:
        result = result * block_scale(rng, extent, pieces, -0.22, 0.18)
    return jnp.clip(result, -most, most).astype(kind)


def setup_inputs(seed: int = 0) -> dict:
    splits = jax.random.split(jax.random.key(seed), 8)
    return {
        "queries": draw_queries(jax.random.fold_in(splits[7], 71), 0),
        "keys": draw_keys(jax.random.fold_in(splits[7], 71), 0),
        "values": scatter_about(splits[2], (SEQUENCE_LENGTH, KEY_VALUE_HEADS * HEAD_SIZE), 1.0, 6.0, ((0, 16), (1, 2))),
        "out_weight": scatter_about(splits[3], (QUERY_HEADS * HEAD_SIZE, D), (QUERY_HEADS * HEAD_SIZE) ** -0.5, 0.09375, ((0, 2),)),
        "residual": scatter_about(splits[4], (SEQUENCE_LENGTH, D), 0.25, 1.5, ((0, 16), (1, 2))),
        "norm_gain": jnp.clip(1.0 + 0.1 * jax.random.normal(splits[5], (D,), jnp.float32), 0.5, 1.5).astype(jnp.bfloat16),
        "span_order": draw_span_order(jax.random.fold_in(splits[7], 71), 0),
    }


def reference(queries, keys, values, out_weight, residual, norm_gain, span_order):
    total_spans = 2 * N_CTX
    span_rows = SEQUENCE_LENGTH // total_spans
    group_size = QUERY_HEADS // KEY_VALUE_HEADS
    scale = 1.0 / math.sqrt(HEAD_SIZE)
    slots = jnp.zeros((total_spans,), jnp.int32).at[span_order].set(jnp.arange(total_spans, dtype=jnp.int32))

    def map_to_positions(array):
        return array.reshape(total_spans, span_rows, array.shape[1])[slots].reshape(SEQUENCE_LENGTH, array.shape[1])
    every_query_row = map_to_positions(queries).astype(jnp.float32).reshape(SEQUENCE_LENGTH, KEY_VALUE_HEADS, group_size, HEAD_SIZE)
    every_key_row = map_to_positions(keys).astype(jnp.float32).reshape(SEQUENCE_LENGTH, KEY_VALUE_HEADS, HEAD_SIZE)
    every_value_row = map_to_positions(values).astype(jnp.float32).reshape(SEQUENCE_LENGTH, KEY_VALUE_HEADS, HEAD_SIZE)
    block_index = min(512, SEQUENCE_LENGTH)
    blocks = SEQUENCE_LENGTH // block_index

    def one_block(number):
        query_block = lax.dynamic_slice_in_dim(every_query_row, number * block_index, block_index, 0)
        query_pos = number * block_index + jnp.arange(block_index, dtype=jnp.int32)

        def step(other, state):
            running, total, accum = state
            key_block = lax.dynamic_slice_in_dim(every_key_row, other * block_index, block_index, 0)
            value_block = lax.dynamic_slice_in_dim(every_value_row, other * block_index, block_index, 0)
            key_pos = other * block_index + jnp.arange(block_index, dtype=jnp.int32)
            scores = jnp.einsum('qhgd,khd->qhgk', query_block, key_block) * scale
            allowed = (key_pos[None, :] <= query_pos[:, None])[:, None, None, :]
            scores = jnp.where(allowed, scores, -1e+30)
            newmax = jnp.maximum(running, lax.optimization_barrier(jnp.max(scores, axis=-1)))
            weights = jnp.where(allowed, jnp.exp(scores - newmax[..., None]), 0.0)
            fade = jnp.exp(running - newmax)
            total = total * fade + lax.optimization_barrier(jnp.sum(weights, axis=-1))
            rounded = lax.optimization_barrier(weights.astype(jnp.bfloat16)).astype(jnp.float32)
            accum = accum * fade[..., None] + jnp.einsum('qhgk,khd->qhgd', rounded, value_block)
            return (newmax, total, accum)
        start_offset = (jnp.full((block_index, KEY_VALUE_HEADS, group_size), -1e+30, jnp.float32), jnp.zeros((block_index, KEY_VALUE_HEADS, group_size), jnp.float32), jnp.zeros((block_index, KEY_VALUE_HEADS, group_size, HEAD_SIZE), jnp.float32))
        running, total, accum = lax.fori_loop(0, number + 1, step, start_offset)
        return accum / total[..., None]
    attended = lax.map(one_block, jnp.arange(blocks, dtype=jnp.int32))
    attended = attended.reshape(SEQUENCE_LENGTH, QUERY_HEADS * HEAD_SIZE).astype(jnp.bfloat16)
    attended = attended.reshape(total_spans, span_rows, QUERY_HEADS * HEAD_SIZE)[span_order].reshape(SEQUENCE_LENGTH, QUERY_HEADS * HEAD_SIZE)
    projected = jnp.dot(attended, out_weight, preferred_element_type=jnp.float32)
    hidden = (residual.astype(jnp.float32) + projected).astype(jnp.bfloat16)
    hidden_f = hidden.astype(jnp.float32)
    meansq = lax.optimization_barrier(jnp.mean(hidden_f * hidden_f, axis=1, keepdims=True))
    normed = hidden_f * lax.rsqrt(meansq + 1e-05) * norm_gain.astype(jnp.float32)[None, :]
    return normed.astype(jnp.bfloat16)
```

```python
import functools
import math

import jax
import jax.numpy as jnp
from jax import lax
from jax.experimental import pallas as pl
from jax.experimental.pallas import tpu as pltpu
from jax.sharding import PartitionSpec as P

HEAD_SIZE = 128
EPSILON = 1e-05
MESH = pl.DeviceIdType.MESH
GROUP = 4


def factor(n):
    bits = n.bit_length() - 1
    if n != 1 << bits:
        return (n, 1, 1)
    inner = bits // 3
    return (1 << (bits - 2 * inner), 1 << inner, 1 << inner)


def pick(index, table):
    value = jnp.int32(table[-1])
    for i in range(len(table) - 1):
        value = jnp.where(index == i, jnp.int32(table[i]), value)
    return value


def nearest(n):
    return [sorted(range(n), key=lambda s: (abs(s - c), s)) for c in range(n)]


def rank_order(sizes, weights):
    ranks = [
        (a, b, c)
        for a in range(sizes[0])
        for b in range(sizes[1])
        for c in range(sizes[2])
    ]
    return sorted(ranks, key=lambda r: (sum(x * w for x, w in zip(r, weights)), r[::-1]))


def kernel(
    n_ctx, n_tp, span_ref, q_hbm, k_hbm, v_hbm, w_hbm, res_hbm, gain_hbm, out_ref,
    kv, q, q_t, bias, acc, top, total, att, w, res, gain, sendbuf, recvbuf, hid, sq_out, sq_in,
    local_sem, send_sem, recv_sem, rs_send, rs_recv, sq_send, sq_recv,
):
    rows = q_hbm.shape[0]
    span_rows = rows // 2
    kv_heads = k_hbm.shape[1] // HEAD_SIZE
    heads = q_hbm.shape[1] // HEAD_SIZE
    group = heads // kv_heads
    lanes = group * rows
    features = res_hbm.shape[1]
    scale2 = math.log2(math.e) / math.sqrt(HEAD_SIZE)
    sizes = factor(n_ctx)
    me = lax.axis_index("ctx")
    tp = lax.axis_index("tp")

    cz = me // (sizes[1] * sizes[2])
    cy = (me // sizes[2]) % sizes[1]
    cx = me % sizes[2]
    odd = tp % 2
    if sizes[1] == sizes[2]:
        ca = cy + odd * (cx - cy)
        cb = cx + odd * (cy - cx)
        sa = sizes[2] + odd * (1 - sizes[2])
        sb = 1 + odd * (sizes[2] - 1)
    else:
        ca, cb, sa, sb = cy, cx, sizes[2], 1
    coords = (cz, ca, cb)
    strides = (sizes[1] * sizes[2], sa, sb)
    near = []
    for d in range(3):
        table = nearest(sizes[d])
        near.append([pick(coords[d], [table[c][r] for c in range(sizes[d])]) for r in range(sizes[d])])

    def neighbours(d):
        n, c, s = sizes[d], coords[d], strides[d]
        if n == 1:
            return []
        if n == 2:
            return [(None, me + (1 - 2 * c) * s)]
        return [(c < n - 1, me + s), (c > 0, me - s)]

    def when(valid, body):
        if valid is None:
            body()
        else:
            pl.when(valid)(body)

    loads = []
    for h in range(kv_heads):
        cols = pl.ds(h * HEAD_SIZE, HEAD_SIZE)
        loads.append(pltpu.make_async_copy(k_hbm.at[:, cols], kv.at[me, h, 0], local_sem.at[2 * h]))
        loads.append(pltpu.make_async_copy(v_hbm.at[:, cols], kv.at[me, h, 1], local_sem.at[2 * h + 1]))
    load_q = pltpu.make_async_copy(q_hbm, q, local_sem.at[2 * kv_heads])
    load_w = pltpu.make_async_copy(w_hbm, w, local_sem.at[2 * kv_heads + 1])
    load_r = pltpu.make_async_copy(res_hbm, res, local_sem.at[2 * kv_heads + 2])
    load_g = pltpu.make_async_copy(gain_hbm, gain, local_sem.at[2 * kv_heads + 3])
    for copy in loads:
        copy.start()
    load_q.start()

    barrier = pltpu.get_barrier_semaphore()
    expected = jnp.int32(n_tp - 1)
    for d in range(3):
        for valid, device in neighbours(d):
            def greet(device=device):
                pl.semaphore_signal(barrier, inc=1, device_id={"ctx": device}, device_id_type=MESH)
            when(valid, greet)
            expected = expected + (1 if valid is None else valid.astype(jnp.int32))
    for j in range(1, n_tp):
        pl.semaphore_signal(barrier, inc=1, device_id={"tp": lax.rem(tp + j, n_tp)}, device_id_type=MESH)
    pl.semaphore_wait(barrier, expected)

    sends = []

    def send(h, src, valid, device):
        slot = len(sends)
        copy = pltpu.make_async_remote_copy(
            src_ref=kv.at[src, h],
            dst_ref=kv.at[src, h],
            send_sem=send_sem.at[slot],
            recv_sem=recv_sem.at[h, src],
            device_id={"ctx": device},
            device_id_type=MESH,
        )
        when(valid, copy.start)
        sends.append((valid, copy))

    last_first = kv_heads // 4
    orders, walks = [], []
    for h in range(kv_heads):
        if h < kv_heads - last_first:
            order, weights = (0, 1, 2), (1.0, 1.1, 2.2)
        else:
            order, weights = (1, 2, 0), (1.0, 1.1, 3.0)
        orders.append(order)
        walks.append(rank_order([sizes[d] for d in order], weights))

    def source(h, ranks):
        src = jnp.int32(0)
        for d, r in zip(orders[h], ranks):
            src = src + near[d][r] * strides[d]
        return src

    def arrive(h, ranks):
        order = orders[h]
        src = source(h, ranks)
        moved = [k for k in range(3) if ranks[k] > 0]
        last = moved[-1] if moved else -1
        if moved:
            pltpu.make_async_copy(kv.at[src, h], kv.at[src, h], recv_sem.at[h, src]).wait()
            d = order[last]
            if sizes[d] > 2:
                c, s = coords[d], near[d][ranks[last]]
                up = (s < c).astype(jnp.int32)
                step = 2 * up - 1
                ahead = c + step
                send(h, src, jnp.logical_and(ahead >= 0, ahead < sizes[d]), me + step * strides[d])
        for k in range(last + 1, 3):
            for valid, device in neighbours(order[k]):
                send(h, src, valid, device)
        return src

    for h in range(kv_heads):
        loads[2 * h].wait()
        loads[2 * h + 1].wait()
        arrive(h, (0, 0, 0))
    load_w.start()
    load_r.start()
    load_g.start()

    row = lax.broadcasted_iota(jnp.int32, (rows, rows), 0)
    lane = lax.broadcasted_iota(jnp.int32, (rows, rows), 1)

    def position(index, device):
        first, second = span_ref[2 * device], span_ref[2 * device + 1]
        return index + jnp.where(index < span_rows, first * span_rows, (second - 1) * span_rows)

    query_pos = position(lane, me)

    @pl.loop(0, n_ctx)
    def _(src):
        bias[src] = jnp.where(position(row, src) <= query_pos, 0.0, -1e30)

    load_q.wait()
    for h in range(heads):
        q_t[h // group, :, (h % group) * rows:(h % group + 1) * rows] = (
            q[:, h * HEAD_SIZE:(h + 1) * HEAD_SIZE].T
        )

    width = min(lanes, 256)

    def attend(h, srcs, first):
        v_t = jnp.concatenate([kv[s, h, 1].T for s in srcs], axis=1)
        keys = [kv[s, h, 0] for s in srcs]
        masks = [jnp.concatenate([bias[s]] * (width // rows), axis=1) for s in srcs]
        for at in range(0, lanes, width):
            cols = pl.ds(at, width)
            qq = q_t[h, :, cols]
            scores = jnp.concatenate(
                [jnp.dot(k, qq, preferred_element_type=jnp.float32) + m for k, m in zip(keys, masks)], axis=0
            )
            new = jnp.max(scores, axis=0, keepdims=True)
            if not first:
                old = top[h, :, cols]
                new = jnp.maximum(old, new)
            weights = jnp.exp2((scores - new) * scale2)
            part = jnp.sum(weights, axis=0, keepdims=True)
            value = jnp.dot(v_t, weights.astype(jnp.bfloat16), preferred_element_type=jnp.float32)
            if not first:
                fade = jnp.exp2((old - new) * scale2)
                part = part + total[h, :, cols] * fade
                value = value + acc[h, :, cols] * fade
            top[h, :, cols] = new
            total[h, :, cols] = part
            acc[h, :, cols] = value

    pending = [[(0, 0, 0)] for _ in range(kv_heads)]
    for p in range(1, n_ctx):
        for h in range(kv_heads):
            arrive(h, walks[h][p])
            pending[h].append(walks[h][p])
            if len(pending[h]) == GROUP or p == n_ctx - 1:
                attend(h, [source(h, r) for r in pending[h]], p < GROUP)
                pending[h] = []

    for h in range(heads):
        cols = pl.ds((h % group) * rows, rows)
        done = acc[h // group, :, cols] / total[h // group, :, cols]
        att[:, h * HEAD_SIZE:(h + 1) * HEAD_SIZE] = done.astype(jnp.bfloat16).T

    chunk = min(features, 512)
    chunks = features // chunk
    load_w.wait()
    att_all = att[...]

    def project(owner, c):
        cols = pl.ds(pl.multiple_of(owner * features + c * chunk, chunk), chunk)
        return jnp.dot(att_all, w[:, cols], preferred_element_type=jnp.float32)

    shares = []
    for j in range(1, n_tp):
        peer = lax.rem(tp + j, n_tp)
        for c in range(chunks):
            sendbuf[j - 1, c] = project(peer, c).astype(jnp.bfloat16)
            copy = pltpu.make_async_remote_copy(
                src_ref=sendbuf.at[j - 1, c],
                dst_ref=recvbuf.at[j - 1, c],
                send_sem=rs_send.at[j - 1, c],
                recv_sem=rs_recv.at[j - 1, c],
                device_id={"tp": peer},
                device_id_type=MESH,
            )
            copy.start()
            shares.append(copy)
    load_r.wait()
    own = [project(tp, c) for c in range(chunks)]
    squares = jnp.zeros((rows, HEAD_SIZE), jnp.float32)
    for c in range(chunks):
        share = own[c]
        for j in range(1, n_tp):
            shares[(j - 1) * chunks + c].wait_recv()
            share = share + recvbuf[j - 1, c].astype(jnp.float32)
        cols = slice(c * chunk, (c + 1) * chunk)
        hidden = (res[:, cols].astype(jnp.float32) + share).astype(jnp.bfloat16)
        hid[:, cols] = hidden
        hidden = hidden.astype(jnp.float32)
        for i in range(0, chunk, HEAD_SIZE):
            piece = hidden[:, i:i + HEAD_SIZE]
            squares = squares + piece * piece
    mine = jnp.sum(squares.T, axis=0, keepdims=True)
    sq_out[...] = jnp.broadcast_to(mine, sq_out.shape)
    last = []
    for j in range(1, n_tp):
        copy = pltpu.make_async_remote_copy(
            src_ref=sq_out,
            dst_ref=sq_in.at[j - 1],
            send_sem=sq_send.at[j - 1],
            recv_sem=sq_recv.at[j - 1],
            device_id={"tp": lax.rem(tp + j, n_tp)},
            device_id_type=MESH,
        )
        copy.start()
        last.append(copy)
    load_g.wait()
    for valid, copy in sends:
        when(valid, copy.wait_send)
    for copy in shares:
        copy.wait_send()
    for j, copy in enumerate(last):
        copy.wait_recv()
        mine = mine + sq_in[j][0:1]
    inverse = lax.rsqrt(mine / (features * n_tp) + EPSILON)
    inverse = jnp.broadcast_to(inverse, (HEAD_SIZE, rows)).T
    for i in range(0, features, HEAD_SIZE):
        cols = slice(i, i + HEAD_SIZE)
        normed = hid[:, cols].astype(jnp.float32) * inverse * gain[:, cols].astype(jnp.float32)
        out_ref[:, cols] = normed.astype(jnp.bfloat16)
    for copy in last:
        copy.wait_send()


def per_device(n_ctx, n_tp, queries, keys, values, out_weight, residual, norm_gain, span_order):
    rows = queries.shape[0]
    heads = queries.shape[1] // HEAD_SIZE
    kv_heads = keys.shape[1] // HEAD_SIZE
    lanes = heads // kv_heads * rows
    features = residual.shape[1]
    chunk = min(features, 512)
    chunks = features // chunk
    peers = max(1, n_tp - 1)
    bf, f32 = jnp.bfloat16, jnp.float32
    hbm = pl.BlockSpec(memory_space=pl.ANY)
    vmem = pltpu.VMEM
    dma = pltpu.SemaphoreType.DMA
    return pl.pallas_call(
        functools.partial(kernel, n_ctx, n_tp),
        out_shape=jax.ShapeDtypeStruct((rows, features), bf),
        in_specs=[pl.BlockSpec(memory_space=pltpu.SMEM)] + [hbm] * 6,
        out_specs=pl.BlockSpec(memory_space=pltpu.VMEM),
        scratch_shapes=[
            vmem((n_ctx, kv_heads, 2, rows, HEAD_SIZE), bf),
            vmem((rows, heads * HEAD_SIZE), bf),
            vmem((kv_heads, HEAD_SIZE, lanes), bf),
            vmem((n_ctx, rows, rows), f32),
            vmem((kv_heads, HEAD_SIZE, lanes), f32),
            vmem((kv_heads, 1, lanes), f32),
            vmem((kv_heads, 1, lanes), f32),
            vmem((rows, heads * HEAD_SIZE), bf),
            vmem(out_weight.shape, bf),
            vmem((rows, features), bf),
            vmem((1, features), bf),
            vmem((peers, chunks, rows, chunk), bf),
            vmem((peers, chunks, rows, chunk), bf),
            vmem((rows, features), bf),
            vmem((8, rows), f32),
            vmem((peers, 8, rows), f32),
            dma((2 * kv_heads + 4,)),
            dma((kv_heads * 6 * n_ctx // 2,)),
            dma((kv_heads, n_ctx)),
            dma((peers, chunks)),
            dma((peers, chunks)),
            dma((peers,)),
            dma((peers,)),
        ],
        compiler_params=pltpu.CompilerParams(
            collective_id=0, has_side_effects=True, vmem_limit_bytes=60 * 1024 * 1024
        ),
    )(span_order, queries, keys, values, out_weight, residual, norm_gain.reshape(1, features))


def solution(mesh):
    return jax.shard_map(
        functools.partial(per_device, mesh.shape["ctx"], mesh.shape["tp"]),
        mesh=mesh,
        in_specs=(
            P("ctx", "tp"),
            P("ctx", "tp"),
            P("ctx", "tp"),
            P("tp", None),
            P("ctx", "tp"),
            P("tp"),
            P(),
        ),
        out_specs=P("ctx", "tp"),
        check_vma=False,
    )
```

```python
import functools
import math

import jax
import jax.numpy as jnp
from jax import lax
from jax.experimental import pallas as pl
from jax.experimental.pallas import tpu as pltpu
from jax.sharding import PartitionSpec as P

HEAD_SIZE = 128
EPSILON = 1e-05
MESH = pl.DeviceIdType.MESH
GROUP = 4


def factor(n):
    bits = n.bit_length() - 1
    if n != 1 << bits:
        return (n, 1, 1)
    inner = bits // 3
    return (1 << (bits - 2 * inner), 1 << inner, 1 << inner)


def pick(index, table):
    value = jnp.int32(table[-1])
    for i in range(len(table) - 1):
        value = jnp.where(index == i, jnp.int32(table[i]), value)
    return value


def nearest(n):
    return [sorted(range(n), key=lambda s: (abs(s - c), s)) for c in range(n)]


def rank_order(sizes, weights):
    ranks = [
        (a, b, c)
        for a in range(sizes[0])
        for b in range(sizes[1])
        for c in range(sizes[2])
    ]
    return sorted(ranks, key=lambda r: (sum(x * w for x, w in zip(r, weights)), r[::-1]))


def kernel(
    n_ctx, n_tp, span_ref, q_hbm, k_hbm, v_hbm, w_hbm, res_hbm, gain_hbm, out_ref,
    kv, q, q_t, bias, acc, top, total, att, w, res, gain, sendbuf, recvbuf, hid, sq_out, sq_in,
    local_sem, send_sem, recv_sem, rs_send, rs_recv, sq_send, sq_recv,
):
    rows = q_hbm.shape[0]
    span_rows = rows // 2
    kv_heads = k_hbm.shape[1] // HEAD_SIZE
    heads = q_hbm.shape[1] // HEAD_SIZE
    group = heads // kv_heads
    lanes = group * rows
    features = res_hbm.shape[1]
    scale2 = math.log2(math.e) / math.sqrt(HEAD_SIZE)
    sizes = factor(n_ctx)
    me = lax.axis_index("ctx")
    tp = lax.axis_index("tp")

    cz = me // (sizes[1] * sizes[2])
    cy = (me // sizes[2]) % sizes[1]
    cx = me % sizes[2]
    odd = tp % 2
    if sizes[1] == sizes[2]:
        ca = cy + odd * (cx - cy)
        cb = cx + odd * (cy - cx)
        sa = sizes[2] + odd * (1 - sizes[2])
        sb = 1 + odd * (sizes[2] - 1)
    else:
        ca, cb, sa, sb = cy, cx, sizes[2], 1
    coords = (cz, ca, cb)
    strides = (sizes[1] * sizes[2], sa, sb)
    near = []
    for d in range(3):
        table = nearest(sizes[d])
        near.append([pick(coords[d], [table[c][r] for c in range(sizes[d])]) for r in range(sizes[d])])

    def neighbours(d):
        n, c, s = sizes[d], coords[d], strides[d]
        if n == 1:
            return []
        if n == 2:
            return [(None, me + (1 - 2 * c) * s)]
        return [(c < n - 1, me + s), (c > 0, me - s)]

    def when(valid, body):
        if valid is None:
            body()
        else:
            pl.when(valid)(body)

    loads = []
    for h in range(kv_heads):
        cols = pl.ds(h * HEAD_SIZE, HEAD_SIZE)
        loads.append(pltpu.make_async_copy(k_hbm.at[:, cols], kv.at[me, h, 0], local_sem.at[2 * h]))
        loads.append(pltpu.make_async_copy(v_hbm.at[:, cols], kv.at[me, h, 1], local_sem.at[2 * h + 1]))
    load_q = pltpu.make_async_copy(q_hbm, q, local_sem.at[2 * kv_heads])
    load_w = pltpu.make_async_copy(w_hbm, w, local_sem.at[2 * kv_heads + 1])
    load_r = pltpu.make_async_copy(res_hbm, res, local_sem.at[2 * kv_heads + 2])
    load_g = pltpu.make_async_copy(gain_hbm, gain, local_sem.at[2 * kv_heads + 3])

    barrier = pltpu.get_barrier_semaphore()
    expected = jnp.int32(n_tp - 1)
    for d in range(3):
        for valid, device in neighbours(d):
            def greet(device=device):
                pl.semaphore_signal(barrier, inc=1, device_id={"ctx": device}, device_id_type=MESH)
            when(valid, greet)
            expected = expected + (1 if valid is None else valid.astype(jnp.int32))
    for j in range(1, n_tp):
        pl.semaphore_signal(barrier, inc=1, device_id={"tp": lax.rem(tp + j, n_tp)}, device_id_type=MESH)
    for copy in loads:
        copy.start()
    load_q.start()
    pl.semaphore_wait(barrier, expected)

    sends = []

    def send(h, src, valid, device):
        slot = len(sends)
        copy = pltpu.make_async_remote_copy(
            src_ref=kv.at[src, h],
            dst_ref=kv.at[src, h],
            send_sem=send_sem.at[slot],
            recv_sem=recv_sem.at[h, src],
            device_id={"ctx": device},
            device_id_type=MESH,
        )
        when(valid, copy.start)
        sends.append((valid, copy))

    last_first = kv_heads // 4
    orders, walks = [], []
    for h in range(kv_heads):
        if h < kv_heads - last_first:
            order, weights = (0, 1, 2), (1.0, 1.1, 2.2)
        else:
            order, weights = (1, 2, 0), (1.0, 1.1, 3.0)
        orders.append(order)
        walks.append(rank_order([sizes[d] for d in order], weights))

    def source(h, ranks):
        src = jnp.int32(0)
        for d, r in zip(orders[h], ranks):
            src = src + near[d][r] * strides[d]
        return src

    def arrive(h, ranks):
        order = orders[h]
        src = source(h, ranks)
        moved = [k for k in range(3) if ranks[k] > 0]
        last = moved[-1] if moved else -1
        if moved:
            pltpu.make_async_copy(kv.at[src, h], kv.at[src, h], recv_sem.at[h, src]).wait()
            d = order[last]
            if sizes[d] > 2:
                c, s = coords[d], near[d][ranks[last]]
                up = (s < c).astype(jnp.int32)
                step = 2 * up - 1
                ahead = c + step
                send(h, src, jnp.logical_and(ahead >= 0, ahead < sizes[d]), me + step * strides[d])
        for k in range(last + 1, 3):
            for valid, device in neighbours(order[k]):
                send(h, src, valid, device)
        return src

    for h in range(kv_heads):
        loads[2 * h].wait()
        loads[2 * h + 1].wait()
        arrive(h, (0, 0, 0))
    load_w.start()
    load_r.start()
    load_g.start()

    row = lax.broadcasted_iota(jnp.int32, (rows, rows), 0)
    lane = lax.broadcasted_iota(jnp.int32, (rows, rows), 1)

    def position(index, device):
        first, second = span_ref[2 * device], span_ref[2 * device + 1]
        return index + jnp.where(index < span_rows, first * span_rows, (second - 1) * span_rows)

    query_pos = position(lane, me)

    @pl.loop(0, n_ctx)
    def _(src):
        bias[src] = jnp.where(position(row, src) <= query_pos, 0.0, -1e30)

    load_q.wait()
    for h in range(heads):
        q_t[h // group, :, (h % group) * rows:(h % group + 1) * rows] = (
            q[:, h * HEAD_SIZE:(h + 1) * HEAD_SIZE].T
        )

    width = min(lanes, 256)

    def attend(h, srcs, first):
        v_t = jnp.concatenate([kv[s, h, 1].T for s in srcs], axis=1)
        keys = [kv[s, h, 0] for s in srcs]
        masks = [jnp.concatenate([bias[s]] * (width // rows), axis=1) for s in srcs]
        for at in range(0, lanes, width):
            cols = pl.ds(at, width)
            qq = q_t[h, :, cols]
            scores = jnp.concatenate(
                [jnp.dot(k, qq, preferred_element_type=jnp.float32) + m for k, m in zip(keys, masks)], axis=0
            )
            new = jnp.max(scores, axis=0, keepdims=True)
            if not first:
                old = top[h, :, cols]
                new = jnp.maximum(old, new)
            weights = jnp.exp2((scores - new) * scale2)
            part = jnp.sum(weights, axis=0, keepdims=True)
            value = jnp.dot(v_t, weights.astype(jnp.bfloat16), preferred_element_type=jnp.float32)
            if not first:
                fade = jnp.exp2((old - new) * scale2)
                part = part + total[h, :, cols] * fade
                value = value + acc[h, :, cols] * fade
            top[h, :, cols] = new
            total[h, :, cols] = part
            acc[h, :, cols] = value

    pending = [[(0, 0, 0)] for _ in range(kv_heads)]
    for p in range(1, n_ctx):
        for h in range(kv_heads):
            arrive(h, walks[h][p])
            pending[h].append(walks[h][p])
            if len(pending[h]) == GROUP or p == n_ctx - 1:
                attend(h, [source(h, r) for r in pending[h]], p < GROUP)
                pending[h] = []

    for h in range(heads):
        cols = pl.ds((h % group) * rows, rows)
        done = acc[h // group, :, cols] / total[h // group, :, cols]
        att[:, h * HEAD_SIZE:(h + 1) * HEAD_SIZE] = done.astype(jnp.bfloat16).T

    chunk = min(features, 512)
    chunks = features // chunk
    load_w.wait()
    att_all = att[...]

    def project(owner, c):
        cols = pl.ds(pl.multiple_of(owner * features + c * chunk, chunk), chunk)
        return jnp.dot(att_all, w[:, cols], preferred_element_type=jnp.float32)

    shares = []
    for j in range(1, n_tp):
        peer = lax.rem(tp + j, n_tp)
        for c in range(chunks):
            sendbuf[j - 1, c] = project(peer, c).astype(jnp.bfloat16)
            copy = pltpu.make_async_remote_copy(
                src_ref=sendbuf.at[j - 1, c],
                dst_ref=recvbuf.at[j - 1, c],
                send_sem=rs_send.at[j - 1, c],
                recv_sem=rs_recv.at[j - 1, c],
                device_id={"tp": peer},
                device_id_type=MESH,
            )
            copy.start()
            shares.append(copy)
    load_r.wait()
    own = [project(tp, c) for c in range(chunks)]
    squares = jnp.zeros((rows, HEAD_SIZE), jnp.float32)
    for c in range(chunks):
        share = own[c]
        for j in range(1, n_tp):
            shares[(j - 1) * chunks + c].wait_recv()
            share = share + recvbuf[j - 1, c].astype(jnp.float32)
        cols = slice(c * chunk, (c + 1) * chunk)
        hidden = (res[:, cols].astype(jnp.float32) + share).astype(jnp.bfloat16)
        hid[:, cols] = hidden
        hidden = hidden.astype(jnp.float32)
        for i in range(0, chunk, HEAD_SIZE):
            piece = hidden[:, i:i + HEAD_SIZE]
            squares = squares + piece * piece
    mine = jnp.sum(squares.T, axis=0, keepdims=True)
    sq_out[...] = jnp.broadcast_to(mine, sq_out.shape)
    last = []
    for j in range(1, n_tp):
        copy = pltpu.make_async_remote_copy(
            src_ref=sq_out,
            dst_ref=sq_in.at[j - 1],
            send_sem=sq_send.at[j - 1],
            recv_sem=sq_recv.at[j - 1],
            device_id={"tp": lax.rem(tp + j, n_tp)},
            device_id_type=MESH,
        )
        copy.start()
        last.append(copy)
    load_g.wait()
    for valid, copy in sends:
        when(valid, copy.wait_send)
    for copy in shares:
        copy.wait_send()
    for j, copy in enumerate(last):
        copy.wait_recv()
        mine = mine + sq_in[j][0:1]
    inverse = lax.rsqrt(mine / (features * n_tp) + EPSILON)
    inverse = jnp.broadcast_to(inverse, (HEAD_SIZE, rows)).T
    for i in range(0, features, HEAD_SIZE):
        cols = slice(i, i + HEAD_SIZE)
        normed = hid[:, cols].astype(jnp.float32) * inverse * gain[cols].astype(jnp.float32)[None, :]
        out_ref[:, cols] = normed.astype(jnp.bfloat16)
    for copy in last:
        copy.wait_send()


def per_device(n_ctx, n_tp, queries, keys, values, out_weight, residual, norm_gain, span_order):
    rows = queries.shape[0]
    heads = queries.shape[1] // HEAD_SIZE
    kv_heads = keys.shape[1] // HEAD_SIZE
    lanes = heads // kv_heads * rows
    features = residual.shape[1]
    chunk = min(features, 512)
    chunks = features // chunk
    peers = max(1, n_tp - 1)
    bf, f32 = jnp.bfloat16, jnp.float32
    hbm = pl.BlockSpec(memory_space=pl.ANY)
    vmem = pltpu.VMEM
    dma = pltpu.SemaphoreType.DMA
    return pl.pallas_call(
        functools.partial(kernel, n_ctx, n_tp),
        out_shape=jax.ShapeDtypeStruct((rows, features), bf),
        in_specs=[pl.BlockSpec(memory_space=pltpu.SMEM)] + [hbm] * 6,
        out_specs=pl.BlockSpec(memory_space=pltpu.VMEM),
        scratch_shapes=[
            vmem((n_ctx, kv_heads, 2, rows, HEAD_SIZE), bf),
            vmem((rows, heads * HEAD_SIZE), bf),
            vmem((kv_heads, HEAD_SIZE, lanes), bf),
            vmem((n_ctx, rows, rows), f32),
            vmem((kv_heads, HEAD_SIZE, lanes), f32),
            vmem((kv_heads, 1, lanes), f32),
            vmem((kv_heads, 1, lanes), f32),
            vmem((rows, heads * HEAD_SIZE), bf),
            vmem(out_weight.shape, bf),
            vmem((rows, features), bf),
            vmem((features,), bf),
            vmem((peers, chunks, rows, chunk), bf),
            vmem((peers, chunks, rows, chunk), bf),
            vmem((rows, features), bf),
            vmem((8, rows), f32),
            vmem((peers, 8, rows), f32),
            dma((2 * kv_heads + 4,)),
            dma((kv_heads * 6 * n_ctx // 2,)),
            dma((kv_heads, n_ctx)),
            dma((peers, chunks)),
            dma((peers, chunks)),
            dma((peers,)),
            dma((peers,)),
        ],
        compiler_params=pltpu.CompilerParams(
            collective_id=0, has_side_effects=True, vmem_limit_bytes=60 * 1024 * 1024
        ),
    )(span_order, queries, keys, values, out_weight, residual, norm_gain)


def solution(mesh):
    return jax.shard_map(
        functools.partial(per_device, mesh.shape["ctx"], mesh.shape["tp"]),
        mesh=mesh,
        in_specs=(
            P("ctx", "tp"),
            P("ctx", "tp"),
            P("ctx", "tp"),
            P("tp", None),
            P("ctx", "tp"),
            P("tp"),
            P(),
        ),
        out_specs=P("ctx", "tp"),
        check_vma=False,
    )
```

```python
import functools
import math

import jax
import jax.numpy as jnp
from jax import lax
from jax.experimental import pallas as pl
from jax.experimental.pallas import tpu as pltpu
from jax.sharding import PartitionSpec as P

HEAD_SIZE = 128
EPSILON = 1e-05
MESH = pl.DeviceIdType.MESH
GROUP = 4


def factor(n):
    bits = n.bit_length() - 1
    if n != 1 << bits:
        return (n, 1, 1)
    inner = bits // 3
    return (1 << (bits - 2 * inner), 1 << inner, 1 << inner)


def pick(index, table):
    value = jnp.int32(table[-1])
    for i in range(len(table) - 1):
        value = jnp.where(index == i, jnp.int32(table[i]), value)
    return value


def nearest(n):
    return [sorted(range(n), key=lambda s: (abs(s - c), s)) for c in range(n)]


def rank_order(sizes, weights):
    ranks = [
        (a, b, c)
        for a in range(sizes[0])
        for b in range(sizes[1])
        for c in range(sizes[2])
    ]
    return sorted(ranks, key=lambda r: (sum(x * w for x, w in zip(r, weights)), r[::-1]))


def kernel(
    n_ctx, n_tp, span_ref, q_hbm, k_hbm, v_hbm, w_hbm, res_hbm, gain_hbm, out_ref,
    kv, q, q_t, bias, acc, top, total, att, w, res, gain, sendbuf, recvbuf, hid, sq_out, sq_in,
    local_sem, send_sem, recv_sem, rs_send, rs_recv, sq_send, sq_recv,
):
    rows = q_hbm.shape[0]
    span_rows = rows // 2
    kv_heads = k_hbm.shape[1] // HEAD_SIZE
    heads = q_hbm.shape[1] // HEAD_SIZE
    group = heads // kv_heads
    lanes = group * rows
    features = res_hbm.shape[1]
    scale2 = math.log2(math.e) / math.sqrt(HEAD_SIZE)
    sizes = factor(n_ctx)
    me = lax.axis_index("ctx")
    tp = lax.axis_index("tp")

    cz = me // (sizes[1] * sizes[2])
    cy = (me // sizes[2]) % sizes[1]
    cx = me % sizes[2]
    odd = tp % 2
    if sizes[1] == sizes[2]:
        ca = cy + odd * (cx - cy)
        cb = cx + odd * (cy - cx)
        sa = sizes[2] + odd * (1 - sizes[2])
        sb = 1 + odd * (sizes[2] - 1)
    else:
        ca, cb, sa, sb = cy, cx, sizes[2], 1
    coords = (cz, ca, cb)
    strides = (sizes[1] * sizes[2], sa, sb)
    near = []
    for d in range(3):
        table = nearest(sizes[d])
        near.append([pick(coords[d], [table[c][r] for c in range(sizes[d])]) for r in range(sizes[d])])

    def neighbours(d):
        n, c, s = sizes[d], coords[d], strides[d]
        if n == 1:
            return []
        if n == 2:
            return [(None, me + (1 - 2 * c) * s)]
        return [(c < n - 1, me + s), (c > 0, me - s)]

    def when(valid, body):
        if valid is None:
            body()
        else:
            pl.when(valid)(body)

    loads = []
    for h in range(kv_heads):
        cols = pl.ds(h * HEAD_SIZE, HEAD_SIZE)
        loads.append(pltpu.make_async_copy(k_hbm.at[:, cols], kv.at[me, h, 0], local_sem.at[2 * h]))
        loads.append(pltpu.make_async_copy(v_hbm.at[:, cols], kv.at[me, h, 1], local_sem.at[2 * h + 1]))
    load_q = pltpu.make_async_copy(q_hbm, q, local_sem.at[2 * kv_heads])
    load_w = pltpu.make_async_copy(w_hbm, w, local_sem.at[2 * kv_heads + 1])
    load_r = pltpu.make_async_copy(res_hbm, res, local_sem.at[2 * kv_heads + 2])
    load_g = pltpu.make_async_copy(gain_hbm, gain, local_sem.at[2 * kv_heads + 3])

    barrier = pltpu.get_barrier_semaphore()
    expected = jnp.int32(n_tp - 1)
    for d in range(3):
        for valid, device in neighbours(d):
            def greet(device=device):
                pl.semaphore_signal(barrier, inc=1, device_id={"ctx": device}, device_id_type=MESH)
            when(valid, greet)
            expected = expected + (1 if valid is None else valid.astype(jnp.int32))
    for j in range(1, n_tp):
        pl.semaphore_signal(barrier, inc=1, device_id={"tp": lax.rem(tp + j, n_tp)}, device_id_type=MESH)
    for copy in loads:
        copy.start()
    load_q.start()
    pl.semaphore_wait(barrier, expected)

    sends = []

    def send(h, src, valid, device):
        slot = len(sends)
        copy = pltpu.make_async_remote_copy(
            src_ref=kv.at[src, h],
            dst_ref=kv.at[src, h],
            send_sem=send_sem.at[slot],
            recv_sem=recv_sem.at[h, src],
            device_id={"ctx": device},
            device_id_type=MESH,
        )
        when(valid, copy.start)
        sends.append((valid, copy))

    last_first = kv_heads // 4
    orders, walks = [], []
    for h in range(kv_heads):
        if h < kv_heads - last_first:
            order, weights = (0, 1, 2), (1.0, 1.1, 2.2)
        else:
            order, weights = (1, 2, 0), (1.0, 1.1, 3.0)
        orders.append(order)
        walks.append(rank_order([sizes[d] for d in order], weights))

    def source(h, ranks):
        src = jnp.int32(0)
        for d, r in zip(orders[h], ranks):
            src = src + near[d][r] * strides[d]
        return src

    def arrive(h, ranks):
        order = orders[h]
        src = source(h, ranks)
        moved = [k for k in range(3) if ranks[k] > 0]
        last = moved[-1] if moved else -1
        if moved:
            pltpu.make_async_copy(kv.at[src, h], kv.at[src, h], recv_sem.at[h, src]).wait()
            d = order[last]
            if sizes[d] > 2:
                c, s = coords[d], near[d][ranks[last]]
                up = (s < c).astype(jnp.int32)
                step = 2 * up - 1
                ahead = c + step
                send(h, src, jnp.logical_and(ahead >= 0, ahead < sizes[d]), me + step * strides[d])
        for k in range(last + 1, 3):
            for valid, device in neighbours(order[k]):
                send(h, src, valid, device)
        return src

    for h in range(kv_heads):
        loads[2 * h].wait()
        loads[2 * h + 1].wait()
        arrive(h, (0, 0, 0))
    load_w.start()
    load_r.start()
    load_g.start()

    row = lax.broadcasted_iota(jnp.int32, (rows, rows), 0)
    lane = lax.broadcasted_iota(jnp.int32, (rows, rows), 1)

    def position(index, device):
        first, second = span_ref[2 * device], span_ref[2 * device + 1]
        return index + jnp.where(index < span_rows, first * span_rows, (second - 1) * span_rows)

    query_pos = position(lane, me)

    @pl.loop(0, n_ctx)
    def _(src):
        bias[src] = jnp.where(position(row, src) <= query_pos, 0.0, -1e30)

    load_q.wait()
    for h in range(heads):
        q_t[h // group, :, (h % group) * rows:(h % group + 1) * rows] = (
            q[:, h * HEAD_SIZE:(h + 1) * HEAD_SIZE].T
        )

    width = min(lanes, 256)

    def attend(h, srcs, first):
        v_t = jnp.concatenate([kv[s, h, 1].T for s in srcs], axis=1)
        keys = [kv[s, h, 0] for s in srcs]
        masks = [jnp.concatenate([bias[s]] * (width // rows), axis=1) for s in srcs]
        for at in range(0, lanes, width):
            cols = pl.ds(at, width)
            qq = q_t[h, :, cols]
            scores = jnp.concatenate(
                [jnp.dot(k, qq, preferred_element_type=jnp.float32) + m for k, m in zip(keys, masks)], axis=0
            )
            new = jnp.max(scores, axis=0, keepdims=True)
            if not first:
                old = top[h, :, cols]
                new = jnp.maximum(old, new)
            weights = jnp.exp2((scores - new) * scale2)
            part = jnp.sum(weights, axis=0, keepdims=True)
            value = jnp.dot(v_t, weights.astype(jnp.bfloat16), preferred_element_type=jnp.float32)
            if not first:
                fade = jnp.exp2((old - new) * scale2)
                part = part + total[h, :, cols] * fade
                value = value + acc[h, :, cols] * fade
            top[h, :, cols] = new
            total[h, :, cols] = part
            acc[h, :, cols] = value

    pending = [[(0, 0, 0)] for _ in range(kv_heads)]
    for p in range(1, n_ctx):
        for h in range(kv_heads):
            arrive(h, walks[h][p])
            pending[h].append(walks[h][p])
            if len(pending[h]) == GROUP or p in (n_ctx - 3, n_ctx - 1):
                attend(h, [source(h, r) for r in pending[h]], len(pending[h]) == p + 1)
                pending[h] = []

    for h in range(heads):
        cols = pl.ds((h % group) * rows, rows)
        done = acc[h // group, :, cols] / total[h // group, :, cols]
        att[:, h * HEAD_SIZE:(h + 1) * HEAD_SIZE] = done.astype(jnp.bfloat16).T

    chunk = min(features, 512)
    chunks = features // chunk
    load_w.wait()
    att_all = att[...]

    def project(owner, c):
        cols = pl.ds(pl.multiple_of(owner * features + c * chunk, chunk), chunk)
        return jnp.dot(att_all, w[:, cols], preferred_element_type=jnp.float32)

    shares = []
    for j in range(1, n_tp):
        peer = lax.rem(tp + j, n_tp)
        for c in range(chunks):
            sendbuf[j - 1, c] = project(peer, c).astype(jnp.bfloat16)
            copy = pltpu.make_async_remote_copy(
                src_ref=sendbuf.at[j - 1, c],
                dst_ref=recvbuf.at[j - 1, c],
                send_sem=rs_send.at[j - 1, c],
                recv_sem=rs_recv.at[j - 1, c],
                device_id={"tp": peer},
                device_id_type=MESH,
            )
            copy.start()
            shares.append(copy)
    load_r.wait()
    own = [project(tp, c) for c in range(chunks)]
    squares = jnp.zeros((rows, HEAD_SIZE), jnp.float32)
    for c in range(chunks):
        share = own[c]
        for j in range(1, n_tp):
            shares[(j - 1) * chunks + c].wait_recv()
            share = share + recvbuf[j - 1, c].astype(jnp.float32)
        cols = slice(c * chunk, (c + 1) * chunk)
        hidden = (res[:, cols].astype(jnp.float32) + share).astype(jnp.bfloat16)
        hid[:, cols] = hidden
        hidden = hidden.astype(jnp.float32)
        for i in range(0, chunk, HEAD_SIZE):
            piece = hidden[:, i:i + HEAD_SIZE]
            squares = squares + piece * piece
    mine = jnp.sum(squares.T, axis=0, keepdims=True)
    sq_out[...] = jnp.broadcast_to(mine, sq_out.shape)
    last = []
    for j in range(1, n_tp):
        copy = pltpu.make_async_remote_copy(
            src_ref=sq_out,
            dst_ref=sq_in.at[j - 1],
            send_sem=sq_send.at[j - 1],
            recv_sem=sq_recv.at[j - 1],
            device_id={"tp": lax.rem(tp + j, n_tp)},
            device_id_type=MESH,
        )
        copy.start()
        last.append(copy)
    load_g.wait()
    for valid, copy in sends:
        when(valid, copy.wait_send)
    for copy in shares:
        copy.wait_send()
    for j, copy in enumerate(last):
        copy.wait_recv()
        mine = mine + sq_in[j][0:1]
    inverse = lax.rsqrt(mine / (features * n_tp) + EPSILON)
    inverse = jnp.broadcast_to(inverse, (HEAD_SIZE, rows)).T
    for i in range(0, features, HEAD_SIZE):
        cols = slice(i, i + HEAD_SIZE)
        normed = hid[:, cols].astype(jnp.float32) * inverse * gain[cols].astype(jnp.float32)[None, :]
        out_ref[:, cols] = normed.astype(jnp.bfloat16)
    for copy in last:
        copy.wait_send()


def per_device(n_ctx, n_tp, queries, keys, values, out_weight, residual, norm_gain, span_order):
    rows = queries.shape[0]
    heads = queries.shape[1] // HEAD_SIZE
    kv_heads = keys.shape[1] // HEAD_SIZE
    lanes = heads // kv_heads * rows
    features = residual.shape[1]
    chunk = min(features, 512)
    chunks = features // chunk
    peers = max(1, n_tp - 1)
    bf, f32 = jnp.bfloat16, jnp.float32
    hbm = pl.BlockSpec(memory_space=pl.ANY)
    vmem = pltpu.VMEM
    dma = pltpu.SemaphoreType.DMA
    return pl.pallas_call(
        functools.partial(kernel, n_ctx, n_tp),
        out_shape=jax.ShapeDtypeStruct((rows, features), bf),
        in_specs=[pl.BlockSpec(memory_space=pltpu.SMEM)] + [hbm] * 6,
        out_specs=pl.BlockSpec(memory_space=pltpu.VMEM),
        scratch_shapes=[
            vmem((n_ctx, kv_heads, 2, rows, HEAD_SIZE), bf),
            vmem((rows, heads * HEAD_SIZE), bf),
            vmem((kv_heads, HEAD_SIZE, lanes), bf),
            vmem((n_ctx, rows, rows), f32),
            vmem((kv_heads, HEAD_SIZE, lanes), f32),
            vmem((kv_heads, 1, lanes), f32),
            vmem((kv_heads, 1, lanes), f32),
            vmem((rows, heads * HEAD_SIZE), bf),
            vmem(out_weight.shape, bf),
            vmem((rows, features), bf),
            vmem((features,), bf),
            vmem((peers, chunks, rows, chunk), bf),
            vmem((peers, chunks, rows, chunk), bf),
            vmem((rows, features), bf),
            vmem((8, rows), f32),
            vmem((peers, 8, rows), f32),
            dma((2 * kv_heads + 4,)),
            dma((kv_heads * 6 * n_ctx // 2,)),
            dma((kv_heads, n_ctx)),
            dma((peers, chunks)),
            dma((peers, chunks)),
            dma((peers,)),
            dma((peers,)),
        ],
        compiler_params=pltpu.CompilerParams(
            collective_id=0, has_side_effects=True, vmem_limit_bytes=60 * 1024 * 1024
        ),
    )(span_order, queries, keys, values, out_weight, residual, norm_gain)


def solution(mesh):
    return jax.shard_map(
        functools.partial(per_device, mesh.shape["ctx"], mesh.shape["tp"]),
        mesh=mesh,
        in_specs=(
            P("ctx", "tp"),
            P("ctx", "tp"),
            P("ctx", "tp"),
            P("tp", None),
            P("ctx", "tp"),
            P("tp"),
            P(),
        ),
        out_specs=P("ctx", "tp"),
        check_vma=False,
    )
```
